128 devices in a mesh: row: 8 (over x, y_lo), col: 16 (over z, y_hi, core).
Axes of the slice: x: 4, y: 4 (y_hi: 2, y_lo: 2; y = y_hi * 2 + y_lo), z: 4, core: 2. Of those that a mesh axis runs over, the one named last changes fastest.
Arguments:
- anomalies: bfloat16 [128, 256, 1024], P('row', 'col'), may hold values from -6 to 6
- kappa: bfloat16 [128, 256], P('row', 'col'), may hold values from 0.039794922 to 0.23925781
- members: int32 [1024], replicated, may hold values from 0 to 7
- months: int32 [1024], replicated, may hold values from 0 to 11
- land: int32 [128, 256], P('row', 'col'), may hold values 0 or 1
Outputs:
- covariance: bfloat16 [32768, 32768], P('row', 'col')
The draws below stay inside these ranges and needn't reach their ends.
All inputs are finite; a program needn't handle non-finite values. No bound on the sum of `land` on one device may be relied on, other than what follows from the above.
Results may differ from the reference program's by a relative error of at most 0.0053.
Values may be sent and summed in bfloat16 or wider, within the bound.
No kernel may reach another device: no remote copies, remote signals or barrier semaphores. Data moves between devices by JAX's collectives and lax.ppermute only.
A program may use at most 128 MiB of HBM per device.

```python
import math
import jax
import jax.numpy as jnp
from jax import lax

LAT = 128
LON = 256
MAPS = 1024
MEMBERS = 8
MONTHS = 12
STEPS = 4
TILE = 2048
GROUPS = 96


def touch_ends(values, stream_key, least, largest):
    longest = values.shape.index(max(values.shape))
    spots = []
    for shift in (0, 1):
        where = [jax.random.randint(jax.random.fold_in(stream_key, axis), (), 0, length) for axis, length in enumerate(values.shape)]
        where[longest] = (where[longest] + shift) % values.shape[longest]
        spots.append(tuple(where))
    return values.at[spots[0]].set(least).at[spots[1]].set(largest)


def shard_levels(stream_key, extent, shards, least, largest):
    def one(position, shards_of):
        steps = jax.random.uniform(jax.random.fold_in(jax.random.fold_in(stream_key, 6), position), (shards_of,), jnp.float32, least / len(shards), largest / len(shards))
        return jnp.repeat(jnp.exp(steps), extent[position] // shards_of).reshape((-1,) + (1,) * (len(extent) - position - 1))

    gain = one(*shards[0])
    for cut in shards[1:]:
        gain = gain * one(*cut)
    return gain


def noise(rng, extent, deviation, bound, pieces=(), kind=jnp.bfloat16):
    loudness = shard_levels(rng, extent, pieces, -0.22, 0.18) if pieces else 1.0
    values = jax.random.normal(rng, extent, jnp.float32) * deviation * loudness
    return jnp.minimum(jnp.maximum(values, -bound), bound).astype(kind)


def setup_inputs(seed: int = 0) -> dict:
    key_of = jax.random.split(jax.random.key(seed), 6)
    return {
        "anomalies": noise(key_of[0], (LAT, LON, MAPS), 1.0, 6.0, ((0, 8), (1, 16))),
        "kappa": jnp.clip(jnp.exp(math.log(0.23925781) - 1.7938024 * jax.random.uniform(key_of[1], (LAT, LON), jnp.float32) ** shard_levels(key_of[1], (LAT, LON), ((0, 8), (1, 16)), -0.2, 0.2)), 0.039794922, 0.23925781).astype(jnp.bfloat16),
        "members": touch_ends(jax.random.randint(key_of[2], (MAPS,), 0, MEMBERS), jax.random.fold_in(key_of[2], 1), 0, MEMBERS - 1).astype(jnp.int32),
        "months": touch_ends(jax.random.randint(key_of[3], (MAPS,), 0, MONTHS), jax.random.fold_in(key_of[3], 1), 0, MONTHS - 1).astype(jnp.int32),
        "land": touch_ends((jax.random.randint(key_of[4], (LAT, LON), 0, 10) < 3).astype(jnp.int32), jax.random.fold_in(key_of[4], 1), 0, 1),
    }


def reference(anomalies, kappa, members, months, land):
    field = anomalies.astype(jnp.float32)
    coeff = kappa.astype(jnp.float32)[:, :, None]
    for step in range(STEPS):
        padded = jnp.pad(field, ((1, 1), (0, 0), (0, 0)))
        beside = padded[2:] + padded[:-2] + (jnp.roll(field, -1, axis=1) + jnp.roll(field, 1, axis=1))
        field = field + coeff * (beside - 4.0 * field)
    groups = members * MONTHS + months
    onehot = (groups[:, None] == jnp.arange(GROUPS, dtype=jnp.int32)[None, :]).astype(jnp.float32)
    flat = field.reshape(LAT * LON, MAPS)
    sums = jnp.dot(flat, onehot, precision=lax.Precision.HIGHEST)
    counts = jnp.maximum(lax.optimization_barrier(jnp.sum(onehot, axis=0)), 1.0)
    back = jnp.dot(sums / counts, onehot.T, precision=lax.Precision.HIGHEST)
    phi = ((jnp.arange(LAT).astype(jnp.float32) + 0.5) / LAT - 0.5) * math.pi
    lat_weight = jnp.sqrt(jnp.cos(phi))
    sea_weight = jnp.where(land == 1, 1.0, 0.5).astype(jnp.float32)
    weights = (sea_weight * lat_weight[:, None]).reshape(LAT * LON, 1)
    centred = ((flat - back) * weights).astype(jnp.bfloat16)
    wide = centred.astype(jnp.float32)
    col_tile = jnp.arange(LAT * LON, dtype=jnp.int32) // TILE

    def tile_row(index):
        rows = lax.dynamic_slice_in_dim(wide, (index * TILE).astype(jnp.int32), TILE, 0)
        block = jnp.dot(rows, wide.T, precision=lax.Precision.HIGHEST) / MAPS
        block = jnp.where(col_tile[None, :] >= index, block, 0.0)
        return block.astype(jnp.bfloat16)
    stacked = lax.map(tile_row, jnp.arange(16, dtype=jnp.int32))
    return stacked.reshape(LAT * LON, LAT * LON)
```

```python
import math

import jax
import jax.numpy as jnp
import numpy as np
from jax import lax
from jax.experimental import pallas as pl
from jax.experimental.pallas import tpu as pltpu
from jax.sharding import Mesh, PartitionSpec as P

LAT = 128
MAPS = 1024
MONTHS = 12
STEPS = 4
TILE = 2048
GROUPS = 96
SIZES = (4, 2, 4, 2, 2)
AXES = ("x", "yl", "z", "yh", "k")
BF16 = jnp.bfloat16
F32 = jnp.float32


def send(array, to):
    pairs = []
    for i in range(math.prod(SIZES)):
        target = to(*(int(v) for v in np.unravel_index(i, SIZES)))
        if target is not None:
            pairs.append((i, int(np.ravel_multi_index(target, SIZES))))
    return lax.ppermute(array, AXES, pairs)


def row_shift(step):
    def to(x, yl, z, yh, k):
        row = 2 * x + yl + step
        return (row // 2, row % 2, z, yh, k) if 0 <= row < 8 else None

    return to


def col_shift(step):
    def to(x, yl, z, yh, k):
        col = (4 * z + 2 * yh + k + step) % 16
        return (x, yl, col // 4, col // 2 % 2, col % 2)

    return to


def x_shift(step):
    return lambda x, yl, z, yh, k: ((x + step) % 4, yl, z, yh, k)


def z_shift(step):
    return lambda x, yl, z, yh, k: (x, yl, (z + step) % 4, yh, k)


def swap_yl(x, yl, z, yh, k):
    return (x, 1 - yl, z, yh, k)


def swap_yh(x, yl, z, yh, k):
    return (x, yl, z, 1 - yh, k)


def swap_core(x, yl, z, yh, k):
    return (x, yl, z, yh, 1 - k)


def turn(cross):
    return lambda x, yl, z, yh, k: ((x + z) % 4, yh, x, yl, k ^ cross)


def smooth(anomalies, kappa):
    kappa = jnp.broadcast_to(kappa[:, :, None], kappa.shape + (128,))
    both = jnp.concatenate([anomalies, kappa], axis=2)
    north = send(both[-STEPS:], row_shift(1))
    south = send(both[:STEPS], row_shift(-1))
    both = jnp.concatenate([north, both, south], axis=0)
    west = send(both[:, -STEPS:], col_shift(1))
    east = send(both[:, :STEPS], col_shift(-1))
    both = jnp.concatenate([west, both, east], axis=1)
    field = both[:, :, :MAPS].astype(F32)
    coeff = both[:, :, MAPS : MAPS + 1].astype(F32)
    for _ in range(STEPS):
        beside = field[2:, 1:-1] + field[:-2, 1:-1] + (field[1:-1, 2:] + field[1:-1, :-2])
        coeff = coeff[1:-1, 1:-1]
        inner = field[1:-1, 1:-1]
        field = inner + coeff * (beside - 4.0 * inner)
    return field


def centre(field, weights, onehot, counts):
    lats, lons, maps = field.shape
    flat = field.reshape(lats * lons, maps)
    sums = jnp.dot(flat, onehot, precision=lax.Precision.HIGHEST)
    back = jnp.dot(sums / counts, onehot.T, precision=lax.Precision.HIGHEST)
    centred = ((flat - back) * weights.reshape(lats * lons, 1)).astype(BF16)
    return centred.reshape(lats, lons, maps)


def ring(piece, across, shift):
    half = piece.shape[0] // 2
    other = send(piece, across)
    before = send(piece, shift(1))
    after = send(piece, shift(-1))
    far0 = send(before[:half], shift(1))
    far1 = send(after[half:], shift(-1))
    before_other = send(other, shift(1))
    after_other = send(other, shift(-1))
    far0_other = send(before_other[:half], shift(1))
    far1_other = send(after_other[half:], shift(-1))
    return [
        (piece, 0, 0, None),
        (before, 3, 0, None),
        (after, 1, 0, None),
        (other, 0, 1, None),
        (far0, 2, 0, 0),
        (far1, 2, 0, 1),
        (before_other, 3, 1, None),
        (after_other, 1, 1, None),
        (far0_other, 2, 1, 0),
        (far1_other, 2, 1, 1),
    ]


BLOCK = 512


def product(lefts, rights, left_at, right_at, top, bottom):
    n_left, n_right = len(lefts), len(rights)
    right_units = [(i, j) for i, (a, _) in enumerate(rights) for j in range(a.shape[0])]
    left_units = []
    for i, (a, part) in enumerate(lefts):
        for h in range(2) if part is None else (part,):
            left_units.append((i, 0 if part is not None else 8 * h, h))

    def body(left_at_ref, right_at_ref, live_ref, *refs):
        left_refs = refs[:n_left]
        right_refs = refs[n_left : n_left + n_right]
        out_ref, rhs, lhs, obuf, in_sem, out_sem = refs[n_left + n_right :]

        def right_copy(u):
            i, j = right_units[u]
            at = pl.multiple_of(right_at_ref[u] * 16, 16)
            return pltpu.make_async_copy(right_refs[i].at[j], rhs.at[:, pl.ds(at, 16)], in_sem.at[u])

        def left_copy(u):
            i, base, h = left_units[u]
            at = pl.multiple_of(left_at_ref[i] * 16, 16)
            return pltpu.make_async_copy(
                left_refs[i].at[pl.ds(base, 8)],
                lhs.at[pl.ds(8 * h, 8), pl.ds(at, 16)],
                in_sem.at[len(right_units) + u],
            )

        first = [u for u in range(len(left_units)) if left_units[u][2] == 0]
        second = [u for u in range(len(left_units)) if left_units[u][2] == 1]
        for u in range(len(right_units)):
            right_copy(u).start()
        for u in first + second:
            left_copy(u).start()
        for u in range(len(right_units)):
            right_copy(u).wait()
        for u in first:
            left_copy(u).wait()
        lats = BLOCK // 256
        steps = 4096 // BLOCK

        def out_copy(s, slot):
            return pltpu.make_async_copy(
                obuf.at[slot], out_ref.at[pl.ds(pl.multiple_of(s * BLOCK, BLOCK), BLOCK)], out_sem.at[slot]
            )

        @pl.loop(0, steps)
        def _(s):
            slot = lax.rem(s, 2)

            @pl.when(s == steps // 2)
            def _():
                for u in second:
                    left_copy(u).wait()

            @pl.when(s >= 2)
            def _():
                out_copy(s - 2, slot).wait()

            live = live_ref[s // (steps // 2)]

            @pl.when(live == 1)
            def _():
                rows = lhs[pl.ds(s * lats, lats)].reshape(BLOCK, MAPS)

                @pl.loop(0, 8)
                def _(n):
                    cols = rhs[n]
                    acc = lax.dot_general(rows, cols, (((1,), (1,)), ((), ())), preferred_element_type=F32)
                    obuf[slot, :, pl.ds(pl.multiple_of(n * 256, 256), 256)] = (acc * (1.0 / MAPS)).astype(BF16)

            @pl.when(live == 0)
            def _():
                obuf[slot] = jnp.zeros((BLOCK, 2048), BF16)

            out_copy(s, slot).start()

        for s in (steps - 2, steps - 1):
            out_copy(s, s % 2).wait()

    smem = pl.BlockSpec(memory_space=pltpu.SMEM)
    anyspace = pl.BlockSpec(memory_space=pl.ANY)
    return pl.pallas_call(
        body,
        out_shape=jax.ShapeDtypeStruct((4096, 2048), BF16),
        in_specs=[smem, smem, smem] + [anyspace] * (n_left + n_right),
        out_specs=anyspace,
        scratch_shapes=[
            pltpu.VMEM((8, 256, MAPS), BF16),
            pltpu.VMEM((16, 256, MAPS), BF16),
            pltpu.VMEM((2, BLOCK, 2048), BF16),
            pltpu.SemaphoreType.DMA((len(right_units) + len(left_units),)),
            pltpu.SemaphoreType.DMA((2,)),
        ],
        compiler_params=pltpu.CompilerParams(vmem_limit_bytes=40 << 20),
        cost_estimate=pl.CostEstimate(flops=2 * 4096 * 2048 * 1024, bytes_accessed=28 << 20, transcendentals=0),
        name="product",
    )(left_at, right_at, jnp.stack([top, bottom]), *[a for a, _ in lefts], *[a for a, _ in rights])


def per_device(anomalies, kappa, members, months, land):
    x, yl, z, yh, k = (lax.axis_index(a) for a in AXES)
    row_index = 2 * x + yl
    col_index = 4 * z + 2 * yh + k
    lat_rows = anomalies.shape[0]
    lat_ids = row_index * lat_rows + jnp.arange(lat_rows, dtype=jnp.int32)
    phi = ((lat_ids.astype(F32) + 0.5) / LAT - 0.5) * math.pi
    lat_weight = jnp.sqrt(jnp.cos(phi))
    sea_weight = jnp.where(land == 1, 1.0, 0.5).astype(F32)
    cell_weight = sea_weight * lat_weight[:, None]
    groups = members * MONTHS + months
    onehot = (groups[:, None] == jnp.arange(GROUPS, dtype=jnp.int32)[None, :]).astype(F32)
    counts = jnp.maximum(jnp.sum(onehot, axis=0), 1.0)
    block = centre(smooth(anomalies, kappa), cell_weight, onehot, counts)

    half = lat_rows // 2
    mine = lax.dynamic_slice_in_dim(block, k * half, half, 0)
    theirs = lax.dynamic_slice_in_dim(block, (1 - k) * half, half, 0)
    turned = jnp.stack([send(mine, turn(0)), send(theirs, turn(1))])
    rights = ring(turned, swap_yl, x_shift)
    lefts = ring(block, swap_yh, z_shift)
    partner = [(send(a, swap_core), dz, dy, part) for a, dz, dy, part in lefts]

    dz = np.array([p[1] for p in lefts] * 2, np.int32)
    dy = np.array([p[2] for p in lefts] * 2, np.int32)
    dk = np.array([0] * len(lefts) + [1] * len(partner), np.int32)
    left_at = 4 * ((z + dz) % 4) + 2 * (yh ^ dy) + (k ^ dk)
    units = [(p, j) for p in rights for j in ((0, 1) if p[3] is None else (p[3],))]
    dx = np.array([p[1] for p, _ in units], np.int32)
    dl = np.array([p[2] for p, _ in units], np.int32)
    dk = np.array([j for _, j in units], np.int32)
    right_at = 4 * ((x + dx - z) % 4) + 2 * (yl ^ dl) + (k ^ dk)
    top = (col_index >= 2 * row_index).astype(jnp.int32)
    bottom = (col_index >= 2 * row_index + 1).astype(jnp.int32)
    return product(
        [(a, part) for a, _, _, part in lefts + partner], [(a, None) for a, _, _, _ in rights], left_at, right_at, top, bottom
    )


def solution(mesh):
    fine = Mesh(mesh.devices.reshape(SIZES), AXES)
    placed = P(("x", "yl"), ("z", "yh", "k"))
    whole = P(("x", "yl"), ("z", "yh", "k"), None)
    return jax.shard_map(
        per_device, mesh=fine, in_specs=(whole, placed, P(), P(), placed), out_specs=placed, check_vma=False
    )
```
